32 devices in a mesh: fsdp: 2 (over y), rows: 8 (over z, core), cols: 2 (over x).
Axes of the slice: x: 2, y: 2, z: 4, core: 2. Of those that a mesh axis runs over, the one named last changes fastest.
Arguments:
- image: bfloat16 [2, 128, 256, 128], P('fsdp', 'rows', 'cols'), may hold values from -6 to 6
- dw_kernel: float32 [7, 7, 128], replicated, may hold values from -0.875 to 0.875
- dw_bias: float32 [128], replicated, may hold values from -3 to 3
- layer_norm_gain: float32 [128], replicated, may hold values from 0.1 to 1.9
- layer_norm_bias: float32 [128], replicated, may hold values from -3 to 3
- w_in: bfloat16 [128, 512], P('fsdp'), may hold values from -0.5 to 0.5
- b_in: float32 [512], replicated, may hold values from -3 to 3
- w_out: bfloat16 [512, 128], P('fsdp'), may hold values from -0.25 to 0.25
- b_out: float32 [128], replicated, may hold values from -3 to 3
- cotangent: bfloat16 [2, 128, 256, 128], P('fsdp', 'rows', 'cols'), may hold values from -60 to 60
Outputs:
- mixed: bfloat16 [2, 128, 256, 128], P('fsdp', 'rows', 'cols')
- d_image: bfloat16 [2, 128, 256, 128], P('fsdp', 'rows', 'cols')
- g_w_in: float32 [128, 512], P('fsdp')
- g_w_out: float32 [512, 128], P('fsdp')
- g_b_in: float32 [512], replicated
- g_kernel: float32 [7, 7, 128], replicated
- g_gain: float32 [128], replicated
The draws below stay inside these ranges and needn't reach their ends.
All inputs are finite; a program needn't handle non-finite values.
Results may differ from the reference program's by a relative error of at most 0.0057.
Values may be sent and summed in bfloat16 or wider, within the bound.
No kernel may reach another device: no remote copies, remote signals or barrier semaphores. Data moves between devices by JAX's collectives and lax.ppermute only.
A program may use at most 64 MiB of HBM per device.

```python
import math
import jax
import jax.numpy as jnp
from jax import lax

C = 128
HID = 512
RH = 16
IMAGES = 2
H = 128
W = 256
N_ROWS = 8


def draw_cotangent(key, part):
    keys = jax.random.split(key, 3)
    shape = (IMAGES, H, W, C)
    base = jnp.clip(jax.random.normal(keys[0], shape, jnp.float32), -6.0, 6.0)
    row_scale = 0.3 * jnp.exp(jax.random.uniform(keys[1], (IMAGES, H, 1, 1), jnp.float32) * math.log(10.0))
    col_scale = 0.3 * jnp.exp(jax.random.uniform(keys[2], (IMAGES, 1, W, 1), jnp.float32) * math.log(10.0))
    return (base * row_scale * col_scale).astype(jnp.bfloat16)


def shard_levels(rng, extent, cuts, least, largest):
    factor_of = 1.0
    for position, blocks in cuts:
        draws = jax.random.uniform(jax.random.fold_in(jax.random.fold_in(rng, 6), position), (blocks,), jnp.float32, least / len(cuts), largest / len(cuts))
        factor_of = factor_of * jnp.repeat(jnp.exp(draws), extent[position] // blocks).reshape((-1,) + (1,) * (len(extent) - 1 - position))
    return factor_of


def normal_values(key, shape, spread, reach, shards=(), dtype=jnp.bfloat16):
    gain = shard_levels(key, shape, shards, -0.22, 0.18) if shards else 1.0
    entries = jax.random.normal(key, shape, jnp.float32) * spread * gain
    return jnp.minimum(jnp.maximum(entries, -reach), reach).astype(dtype)


def setup_inputs(seed: int = 0) -> dict:
    splits = jax.random.split(jax.random.key(seed), 11)
    image = normal_values(splits[0], (IMAGES, H, W, C), 1.0, 6.0, ((0, 2), (1, 8), (2, 2)))
    dw_kernel = normal_values(splits[1], (7, 7, C), 49 ** -0.5, 0.875, (), jnp.float32)
    dw_bias = normal_values(splits[2], (C,), 0.5, 3.0, (), jnp.float32)
    layer_norm_gain = jnp.clip(1.0 + 0.18 * jax.random.normal(splits[3], (C,), jnp.float32), 0.1, 1.9)
    layer_norm_bias = normal_values(splits[4], (C,), 0.5, 3.0, (), jnp.float32)
    w_in = normal_values(splits[5], (C, HID), C ** -0.5, 0.5, ((0, 2),))
    b_in = normal_values(splits[6], (HID,), 0.5, 3.0, (), jnp.float32)
    w_out = normal_values(splits[7], (HID, C), HID ** -0.5, 0.25, ((0, 2),))
    b_out = normal_values(splits[8], (C,), 0.5, 3.0, (), jnp.float32)
    cotangent = draw_cotangent(jax.random.fold_in(splits[10], 71), 0)
    return dict(image=image, dw_kernel=dw_kernel, dw_bias=dw_bias, layer_norm_gain=layer_norm_gain, layer_norm_bias=layer_norm_bias, w_in=w_in, b_in=b_in, w_out=w_out, b_out=b_out, cotangent=cotangent)


norm_eps = 1e-06
gelu_coef = math.sqrt(2.0 / math.pi)
cubic_coef = 0.044715

def depthwise_taps(padded, kernel, height, width):
    total = jnp.zeros((height, width, padded.shape[2]), jnp.float32)
    for row_tap in range(7):
        for col_tap in range(7):
            total = total + padded[row_tap:row_tap + height, col_tap:col_tap + width] * kernel[row_tap, col_tap]
    return total

def transposed_taps(padded, kernel, height, width):
    total = jnp.zeros((height, width, padded.shape[2]), jnp.float32)
    for row_tap in range(7):
        for col_tap in range(7):
            total = total + padded[6 - row_tap:6 - row_tap + height, 6 - col_tap:6 - col_tap + width] * kernel[row_tap, col_tap]
    return total

def gelu_parts(pre):
    inner = gelu_coef * (pre + cubic_coef * pre * pre * pre)
    tanh_val = jnp.tanh(inner)
    value = 0.5 * pre * (1.0 + tanh_val)
    slope = 0.5 * (1.0 + tanh_val) + 0.5 * pre * (1.0 - tanh_val * tanh_val) * gelu_coef * (1.0 + 3.0 * cubic_coef * pre * pre)
    return (value, slope)

def reference(image, dw_kernel, dw_bias, layer_norm_gain, layer_norm_bias, w_in, b_in, w_out, b_out, cotangent):
    contract_rows = (((0,), (0,)), ((), ()))
    contract_cols = (((1,), (1,)), ((), ()))

    def per_image(pair):
        field, upstream = pair
        padded_f = jnp.pad(field.astype(jnp.float32), ((3, 3), (3, 3), (0, 0)))
        conv = depthwise_taps(padded_f, dw_kernel, H, W) + dw_bias
        center = lax.optimization_barrier(jnp.mean(conv, axis=-1, keepdims=True))
        variance_spread = conv - center
        inverse_deviation = lax.rsqrt(lax.optimization_barrier(jnp.mean(variance_spread * variance_spread, axis=-1, keepdims=True)) + norm_eps)
        standardized_input = variance_spread * inverse_deviation
        normalized_input = (standardized_input * layer_norm_gain + layer_norm_bias).astype(jnp.bfloat16)

        def per_block(block):
            normed_b, field_b, up_b = block
            pre = jnp.dot(normed_b, w_in, preferred_element_type=jnp.float32) + b_in
            value, slope = gelu_parts(pre)
            hidden = value.astype(jnp.bfloat16)
            mixed_b = (field_b.astype(jnp.float32) + jnp.dot(hidden, w_out, preferred_element_type=jnp.float32) + b_out).astype(jnp.bfloat16)
            d_hidden = lax.dot_general(up_b, w_out, contract_cols, preferred_element_type=jnp.float32)
            d_pre = (d_hidden * slope).astype(jnp.bfloat16)
            normalized_gradient = lax.dot_general(d_pre, w_in, contract_cols, preferred_element_type=jnp.float32)
            term_in = lax.dot_general(normed_b, d_pre, contract_rows, preferred_element_type=jnp.float32)
            term_out = lax.dot_general(hidden, up_b, contract_rows, preferred_element_type=jnp.float32)
            term_bias = lax.optimization_barrier(jnp.sum(d_pre.astype(jnp.float32), axis=0))
            return (mixed_b, normalized_gradient, term_in, term_out, term_bias)
        blocks = lax.map(per_block, (normalized_input.reshape(N_ROWS, RH * W, C), field.reshape(N_ROWS, RH * W, C), upstream.reshape(N_ROWS, RH * W, C)))
        mixed = blocks[0].reshape(H, W, C)
        normalized_gradient = blocks[1].reshape(H, W, C)
        gain_product = lax.optimization_barrier(jnp.sum(normalized_gradient * standardized_input, axis=(0, 1)))
        centered_scaled_gradient = normalized_gradient * layer_norm_gain
        convolution_gradient = (inverse_deviation * (centered_scaled_gradient - lax.optimization_barrier(jnp.mean(centered_scaled_gradient, axis=-1, keepdims=True)) - standardized_input * lax.optimization_barrier(jnp.mean(centered_scaled_gradient * standardized_input, axis=-1, keepdims=True)))).astype(jnp.bfloat16)
        conv_grad = convolution_gradient.astype(jnp.float32)
        grad_padded = jnp.pad(conv_grad, ((3, 3), (3, 3), (0, 0)))
        d_image = (upstream.astype(jnp.float32) + transposed_taps(grad_padded, dw_kernel, H, W)).astype(jnp.bfloat16)
        kernel_rows = []
        for row_tap in range(7):
            for col_tap in range(7):
                kernel_rows.append(lax.optimization_barrier(jnp.sum(padded_f[row_tap:row_tap + H, col_tap:col_tap + W] * conv_grad, axis=(0, 1))))
        kernel_term = jnp.stack(kernel_rows).reshape(7, 7, C)
        return (mixed, d_image, lax.optimization_barrier(jnp.sum(blocks[2], axis=0)), lax.optimization_barrier(jnp.sum(blocks[3], axis=0)), lax.optimization_barrier(jnp.sum(blocks[4], axis=0)), kernel_term, gain_product)
    results = lax.map(per_image, (image, cotangent))
    return (results[0], results[1], lax.optimization_barrier(jnp.sum(results[2], axis=0)), lax.optimization_barrier(jnp.sum(results[3], axis=0)), lax.optimization_barrier(jnp.sum(results[4], axis=0)), lax.optimization_barrier(jnp.sum(results[5], axis=0)), lax.optimization_barrier(jnp.sum(results[6], axis=0)))
```

```python
import functools
import math

import jax
import jax.numpy as jnp
from jax import lax
from jax.experimental import pallas as pl
from jax.experimental.pallas import tpu as pltpu
from jax.sharding import PartitionSpec as P

norm_eps = 1e-06
gelu_coef = math.sqrt(2.0 / math.pi)
cubic_coef = 0.044715
EDGE = 8
F32 = jnp.float32
BF16 = jnp.bfloat16
VMEM = pl.BlockSpec(memory_space=pltpu.VMEM)


def pair_perm(count, first):
    perm = []
    for i in range(first, count - 1, 2):
        perm += [(i, i + 1), (i + 1, i)]
    return perm


def call(kernel, out_shape, scratch=(), cost=None, limit=40 << 20):
    return pl.pallas_call(
        kernel,
        out_shape=out_shape,
        scratch_shapes=scratch,
        compiler_params=pltpu.CompilerParams(vmem_limit_bytes=limit),
        cost_estimate=cost,
    )


def odd(axis):
    return lax.rem(lax.axis_index(axis), 2) == 1


def pick(cond, yes, no):
    return jnp.where(cond, yes.astype(F32), no.astype(F32)).astype(yes.dtype)


def pack_first(image_ref, w_in_ref, w_out_ref, w_pack_ref, *col_refs):
    width = image_ref.shape[1]
    depth, hid = w_in_ref.shape
    for i in range(hid // 128):
        w_pack_ref[i * depth : (i + 1) * depth, :] = w_in_ref[:, i * 128 : (i + 1) * 128]
    w_pack_ref[depth * hid // 128 :, :] = w_out_ref[...]
    pack_cols(image_ref, col_refs)


def pack_cols(field_ref, col_refs):
    width = field_ref.shape[1]
    is_odd = odd("cols")
    left = field_ref[:, 0:EDGE, :]
    right = field_ref[:, width - EDGE : width, :]
    col_refs[0][...] = pick(is_odd, left, right)
    if len(col_refs) > 1:
        col_refs[1][...] = pick(is_odd, right, left)


def col_sides(col_refs):
    is_odd = odd("cols")
    got_a = col_refs[0][...]
    got_b = col_refs[1][...] if len(col_refs) > 1 else jnp.zeros_like(got_a)
    return pick(is_odd, got_a, got_b), pick(is_odd, got_b, got_a)


def pack_rows(n_col, field_ref, *refs):
    col_refs, (row_a, row_b) = refs[:n_col], refs[n_col:]
    height, width, _ = field_ref.shape
    left, right = col_sides(col_refs)
    is_odd = odd("rows")
    for ref, want_top in ((row_a, is_odd), (row_b, jnp.logical_not(is_odd))):
        ref[:, 0:EDGE, :] = pick(want_top, left[0:3], left[height - 3 :])
        ref[:, EDGE : EDGE + width, :] = pick(want_top, field_ref[0:3], field_ref[height - 3 :])
        ref[:, EDGE + width :, :] = pick(want_top, right[0:3], right[height - 3 :])


def fill_padded(padded, field_ref, col_refs, row_a, row_b):
    height, width, _ = field_ref.shape
    left, right = col_sides(col_refs)
    is_odd = odd("rows")
    padded[3 : 3 + height, 0:EDGE, :] = left.astype(F32)
    padded[3 : 3 + height, EDGE + width :, :] = right.astype(F32)

    def row(i, _):
        padded[3 + i, EDGE : EDGE + width, :] = field_ref[i].astype(F32)
        return 0

    lax.fori_loop(0, height, row, 0)
    got_a, got_b = row_a[...].astype(F32), row_b[...].astype(F32)
    padded[0:3] = jnp.where(is_odd, got_a, got_b)
    padded[3 + height :] = jnp.where(is_odd, got_b, got_a)


def taps_of_row(padded, kernel_ref, row, width, flip):
    total = None
    for a in range(7):
        for b in range(7):
            tap = (6 - a) * 7 + 6 - b if flip else a * 7 + b
            term = padded[row + a, pl.ds(EDGE - 3 + b, width), :] * kernel_ref[tap : tap + 1, :]
            total = term if total is None else total + term
    return total


def main_kernel(n_col, rows_at_once, *refs):
    image_ref = refs[0]
    col_refs = refs[1 : 1 + n_col]
    (
        row_a, row_b, kernel_ref, dw_bias_ref, gain_ref, bias_ref, w_in_ref, b_in_ref, w_out_ref,
        b_out_ref, w_got_ref, cot_ref,
        mixed_ref, dconv_ref, own_ref, other_ref,
    ) = refs[1 + n_col : 17 + n_col]
    outs = refs[17 + n_col :]
    dcol_refs = outs[:n_col]
    padded, full_in, full_out, sum_in, sum_out, sum_bias, sum_gain = outs[n_col:]
    height, width, chan = image_ref.shape
    hid = w_in_ref.shape[1]
    in_rows, out_rows = w_in_ref.shape[0], w_out_ref.shape[0]
    me = lax.axis_index("fsdp")
    fill_padded(padded, image_ref, col_refs, row_a, row_b)

    def at(which, size):
        return pl.ds(pl.multiple_of(which * size, size), size)

    full_in[at(me, in_rows), :] = w_in_ref[...]
    for i in range(hid // 128):
        full_in[at(1 - me, in_rows), i * 128 : (i + 1) * 128] = w_got_ref[
            i * in_rows : (i + 1) * in_rows, :
        ]
    full_out[at(me, out_rows), :] = w_out_ref[...]
    full_out[at(1 - me, out_rows), :] = w_got_ref[in_rows * hid // 128 :, :]
    sum_in[...] = jnp.zeros_like(sum_in)
    sum_out[...] = jnp.zeros_like(sum_out)
    sum_bias[...] = jnp.zeros_like(sum_bias)
    sum_gain[...] = jnp.zeros_like(sum_gain)
    gain = gain_ref[...]
    pixels = rows_at_once * width
    half = hid // 2
    nn = (((1,), (0,)), ((), ()))
    nt = (((1,), (1,)), ((), ()))
    tn = (((0,), (0,)), ((), ()))

    def dot(x, y, dims):
        return lax.dot_general(x, y, dims, preferred_element_type=F32)

    def block(i, _):
        first = i * rows_at_once
        conv = jnp.concatenate(
            [
                taps_of_row(padded, kernel_ref, first + j, width, False)
                for j in range(rows_at_once)
            ],
            axis=0,
        ) + dw_bias_ref[...]
        center = jnp.mean(conv, axis=-1, keepdims=True)
        spread = conv - center
        rstd = lax.rsqrt(jnp.mean(spread * spread, axis=-1, keepdims=True) + norm_eps)
        xhat = spread * rstd
        normed = (xhat * gain + bias_ref[...]).astype(BF16)
        upstream = cot_ref[pl.ds(first, rows_at_once)].reshape(pixels, chan)
        field = image_ref[pl.ds(first, rows_at_once)].reshape(pixels, chan)
        mixed = field.astype(F32) + b_out_ref[...]
        back = jnp.zeros((pixels, chan), F32)
        ones = jnp.ones((8, pixels), BF16)
        for h in range(2):
            cols = slice(h * half, (h + 1) * half)
            wi, wo = full_in[:, cols], full_out[cols, :]
            pre = dot(normed, wi, nn) + b_in_ref[:, cols]
            square = pre * pre
            tanh = jnp.tanh(pre * (gelu_coef + (gelu_coef * cubic_coef) * square))
            up_tanh = 1.0 + tanh
            half_pre = 0.5 * pre
            hidden = (half_pre * up_tanh).astype(BF16)
            slope = up_tanh * (
                0.5
                + half_pre
                * (1.0 - tanh)
                * (gelu_coef + (3.0 * gelu_coef * cubic_coef) * square)
            )
            mixed = mixed + dot(hidden, wo, nn)
            d_pre = (dot(upstream, wo, nt) * slope).astype(BF16)
            back = back + dot(d_pre, wi, nt)
            sum_in[:, cols] += dot(normed, d_pre, tn)
            sum_out[:, cols] += dot(upstream, hidden, tn)
            sum_bias[:, cols] += dot(ones, d_pre, nn)
        mixed_ref[pl.ds(first, rows_at_once)] = mixed.astype(BF16).reshape(rows_at_once, width, chan)
        sum_gain[...] += jnp.sum((back * xhat).reshape(pixels // 8, 8, chan), axis=0)
        q = back * gain
        d_conv = rstd * (
            q
            - jnp.mean(q, axis=-1, keepdims=True)
            - xhat * jnp.mean(q * xhat, axis=-1, keepdims=True)
        )
        dconv_ref[pl.ds(first, rows_at_once)] = d_conv.astype(BF16).reshape(
            rows_at_once, width, chan
        )
        return 0

    lax.fori_loop(0, height // rows_at_once, block, 0)
    pack_cols(dconv_ref, dcol_refs)

    base = in_rows * hid // 128 + out_rows
    for ref, which in ((own_ref, me), (other_ref, 1 - me)):
        for i in range(hid // 128):
            ref[i * in_rows : (i + 1) * in_rows, :] = sum_in[
                at(which, in_rows), i * 128 : (i + 1) * 128
            ].astype(BF16)
        ref[in_rows * hid // 128 : base, :] = (
            sum_out[:, at(which, out_rows)].T.astype(BF16)
        )
    small = [sum_bias[0:1, i * 128 : (i + 1) * 128] for i in range(hid // 128)]
    small.append(jnp.sum(sum_gain[...], axis=0, keepdims=True))
    for a in range(7):

        def row(r, sums):
            grad = dconv_ref[r].astype(F32)
            return tuple(
                sums[b]
                + jnp.sum(
                    (padded[r + a, pl.ds(EDGE - 3 + b, width), :] * grad).reshape(
                        width // 8, 8, chan
                    ),
                    axis=0,
                )
                for b in range(7)
            )

        sums = lax.fori_loop(0, height, row, (jnp.zeros((8, chan), F32),) * 7)
        small += [jnp.sum(s, axis=0, keepdims=True) for s in sums]
    small = jnp.concatenate(small, axis=0)
    pad = own_ref.shape[0] - base - small.shape[0]
    small = jnp.concatenate([small, jnp.zeros((pad, chan), F32)], axis=0).astype(BF16)
    own_ref[base:, :] = small
    other_ref[base:, :] = small


def image_kernel(n_col, *refs):
    dconv_ref = refs[0]
    col_refs = refs[1 : 1 + n_col]
    row_a, row_b, kernel_ref, cot_ref, out_ref, padded = refs[1 + n_col :]
    height, width, _ = dconv_ref.shape
    fill_padded(padded, dconv_ref, col_refs, row_a, row_b)

    def row(r, _):
        total = taps_of_row(padded, kernel_ref, r, width, True)
        out_ref[r] = (cot_ref[r].astype(F32) + total).astype(BF16)
        return 0

    lax.fori_loop(0, height, row, 0)


def finish_kernel(acc_ref, got_ref, g_in_ref, g_out_ref, g_b_ref, g_k_ref, g_gain_ref):
    in_rows, hid = g_in_ref.shape
    total = acc_ref[...].astype(F32) + got_ref[...].astype(F32)
    for i in range(hid // 128):
        g_in_ref[:, i * 128 : (i + 1) * 128] = total[i * in_rows : (i + 1) * in_rows]
    base = in_rows * hid // 128
    g_out_ref[...] = total[base : base + g_out_ref.shape[0]]
    base += g_out_ref.shape[0]
    for i in range(hid // 128):
        g_b_ref[:, i * 128 : (i + 1) * 128] = total[base + i : base + i + 1]
    base += hid // 128
    g_gain_ref[...] = total[base : base + 1]
    for a in range(7):
        g_k_ref[a] = total[base + 1 + 7 * a : base + 8 + 7 * a]


def on_device(sizes, image, dw_kernel, dw_bias, gain, bias, w_in, b_in, w_out, b_out, cotangent):
    n_fsdp, n_rows, n_cols = sizes
    field, upstream = image[0], cotangent[0]
    height, width, chan = field.shape
    in_rows, hid = w_in.shape
    out_rows = w_out.shape[0]
    shape = jax.ShapeDtypeStruct
    n_col = 2 if n_cols > 2 else 1
    col_shape = shape((height, EDGE, chan), BF16)
    row_shape = shape((3, width + 2 * EDGE, chan), BF16)
    field_shape = shape((height, width, chan), BF16)
    taps = dw_kernel.reshape(49, chan)

    def swap_cols(edges):
        return [lax.ppermute(e, "cols", pair_perm(n_cols, i)) for i, e in enumerate(edges)]

    def swap_rows(edges):
        return [lax.ppermute(e, "rows", pair_perm(n_rows, i)) for i, e in enumerate(edges)]

    w_rows = in_rows * hid // 128 + out_rows
    w_pack, *cols = call(pack_first, (shape((w_rows, 128), BF16),) + (col_shape,) * n_col)(
        field, w_in, w_out
    )
    cols = swap_cols(cols)
    w_got = lax.ppermute(w_pack, "fsdp", pair_perm(n_fsdp, 0))
    rows = call(functools.partial(pack_rows, n_col), (row_shape,) * 2)(field, *cols)
    rows = swap_rows(rows)
    n_small = hid // 128 + 1 + 49
    pack_shape = shape((w_rows + -(-n_small // 16) * 16, 128), BF16)
    padded = pltpu.VMEM((height + 6, width + 2 * EDGE, chan), F32)
    row1 = lambda v: v.reshape(1, -1)
    mixed, d_conv, own, other, *d_cols = call(
        functools.partial(main_kernel, n_col, 2),
        (field_shape, field_shape, pack_shape, pack_shape) + (col_shape,) * n_col,
        scratch=[
            padded,
            pltpu.VMEM((in_rows * n_fsdp, hid), BF16),
            pltpu.VMEM((out_rows * n_fsdp, chan), BF16),
            pltpu.VMEM((chan, hid), F32),
            pltpu.VMEM((chan, hid), F32),
            pltpu.VMEM((8, hid), F32),
            pltpu.VMEM((8, chan), F32),
        ],
    )(
        field, *cols, *rows, taps, row1(dw_bias), row1(gain), row1(bias), w_in, row1(b_in), w_out,
        row1(b_out), w_got, upstream,
    )
    d_cols = swap_cols(d_cols)
    d_rows = call(functools.partial(pack_rows, n_col), (row_shape,) * 2)(d_conv, *d_cols)
    d_rows = swap_rows(d_rows)
    d_image = call(functools.partial(image_kernel, n_col), field_shape, scratch=[padded])(
        d_conv, *d_cols, *d_rows, taps, upstream
    )

    got = lax.ppermute(other, "fsdp", pair_perm(n_fsdp, 0))
    acc = own
    bits = [("cols", 1 << i) for i in range(n_cols.bit_length() - 1)]
    bits += [("rows", 1 << i) for i in range(n_rows.bit_length() - 1)]
    for axis, bit in bits:
        acc = (acc.astype(F32) + got.astype(F32)).astype(BF16)
        count = n_rows if axis == "rows" else n_cols
        got = lax.ppermute(acc, axis, [(i, i ^ bit) for i in range(count)])
    g_in, g_out, g_b, g_k, g_gain = call(
        finish_kernel,
        (
            shape((in_rows, hid), F32),
            shape((out_rows, chan), F32),
            shape((1, hid), F32),
            shape((7, 7, chan), F32),
            shape((1, chan), F32),
        ),
    )(acc, got)
    return (
        mixed[None], d_image[None], g_in, g_out, g_b.reshape(-1), g_k, g_gain.reshape(-1),
    )


def solution(mesh):
    sizes = tuple(mesh.shape[name] for name in ("fsdp", "rows", "cols"))
    if sizes[0] != 2 or any(n & (n - 1) for n in sizes):
        raise ValueError(sizes)
    blocks = P("fsdp", "rows", "cols", None)
    return jax.shard_map(
        functools.partial(on_device, sizes),
        mesh=mesh,
        in_specs=(
            blocks, P(), P(), P(), P(), P("fsdp", None), P(), P("fsdp", None), P(), blocks,
        ),
        out_specs=(blocks, blocks, P("fsdp", None), P("fsdp", None), P(), P(), P()),
        check_vma=False,
    )
```
